32 devices in a mesh: tm: 4 (over x, core), lat: 8 (over z, y).
Axes of the slice: x: 2, y: 2, z: 4, core: 2. Of those that a mesh axis runs over, the one named last changes fastest.
Arguments:
- states: float32 [32, 512, 256], P('tm', 'lat'), may hold values from -6 to 6
- multipliers: float32 [32, 512, 256], P('tm', 'lat'), may hold values from -3 to 3
- diffusivity: float32 [512, 256], P('lat'), may hold values from 0.02 to 0.15
- zonal_speed: float32 [512, 256], P('lat'), may hold values from -0.3 to 0.3
- meridional_speed: float32 [512, 256], P('lat'), may hold values from -0.3 to 0.3
- observed_cells: int32 [32, 8, 1024], P('tm', 'lat'), may hold values from 0 to 16383
- observed_values: float32 [32, 8, 1024], P('tm', 'lat'), may hold values from -6 to 6
- observed_weights: float32 [32, 8, 1024], P('tm', 'lat'), may hold values from 0.2 to 2
- fresh_cells: int32 [4, 8, 1024], P(None, 'lat'), may hold values from 0 to 16383
- fresh_values: float32 [4, 8, 1024], P(None, 'lat'), may hold values from -6 to 6
- fresh_weights: float32 [4, 8, 1024], P(None, 'lat'), may hold values from 0.2 to 2
Outputs:
- analysis: float32 [32, 512, 256], P('tm', 'lat')
- lagrange: float32 [32, 512, 256], P('tm', 'lat')
The draws below stay inside these ranges and needn't reach their ends.
Inputs may be any that keep to these rules, and one draw needn't show every extreme that they name: `observed_cells`: each entry names a cell of its band, counted row by row over the band's 64 x 256 cells; cells may repeat. `fresh_cells`: each entry names a cell of its band, counted row by row over the band's 64 x 256 cells; cells may repeat.
All inputs are finite; a program needn't handle non-finite values.
Results may differ from the reference program's by a relative error of at most 0.000059.
Values sent between devices are 32-bit elements; how exact they have to be, the bound alone decides.
No kernel may reach another device: no remote copies, remote signals or barrier semaphores. Data moves between devices by JAX's collectives and lax.ppermute only.
A program may use at most 64 MiB of HBM per device.

```python
import math
import jax
import jax.numpy as jnp

ROWS = 64
LON = 256
NOBS = 1024
SWEEPS = 2
HALF = 4
TIMES = 32
NLAT = 512
N_LAT = 8


def place_ends(array, own_key, smallest, top_value):
    spot = [jax.random.randint(jax.random.fold_in(own_key, axis), (), 0, length) for axis, length in enumerate(array.shape)]
    main_axis = array.shape.index(max(array.shape))
    neighbour = spot[:main_axis] + [(spot[main_axis] + 1) % array.shape[main_axis]] + spot[main_axis + 1:]
    return array.at[tuple(spot)].set(smallest).at[tuple(neighbour)].set(top_value)


def level_of(rng, extent, cuts, least, largest):
    def one(axis_at, parts):
        steps = jax.random.uniform(jax.random.fold_in(jax.random.fold_in(rng, 6), axis_at), (parts,), jnp.float32, least / len(cuts), largest / len(cuts))
        return jnp.repeat(jnp.exp(steps), extent[axis_at] // parts).reshape((-1,) + (1,) * (len(extent) - axis_at - 1))

    factor_of = one(*cuts[0])
    for cut in cuts[1:]:
        factor_of = factor_of * one(*cut)
    return factor_of


def centred(key, extent, scale, limit, pieces=(), kind=jnp.bfloat16):
    values = jax.random.normal(key, extent, jnp.float32) * scale
    if len(pieces) > 0:
        values = level_of(key, extent, pieces, -0.22, 0.18) * values
    return jnp.clip(values, min=-limit, max=limit).astype(kind)


def setup_inputs(seed: int = 0) -> dict:
    key_list = jax.random.split(jax.random.key(seed), 12)
    return {
        "states": centred(key_list[0], (TIMES, NLAT, LON), 1.0, 6.0, ((0, 4), (1, 8)), jnp.float32),
        "multipliers": centred(key_list[1], (TIMES, NLAT, LON), 0.5, 3.0, ((0, 4), (1, 8)), jnp.float32),
        "diffusivity": jnp.clip(0.02 + 0.13000001 * jax.random.uniform(key_list[2], (NLAT, LON), jnp.float32) ** level_of(key_list[2], (NLAT, LON), ((0, 8),), -0.2, 0.2), 0.02, 0.15),
        "zonal_speed": jnp.clip(jax.random.uniform(key_list[3], (NLAT, LON), jnp.float32, -0.3, 0.3) * level_of(key_list[3], (NLAT, LON), ((0, 8),), -0.4, 0.0), -0.3, 0.3),
        "meridional_speed": jnp.clip(jax.random.uniform(key_list[4], (NLAT, LON), jnp.float32, -0.3, 0.3) * level_of(key_list[4], (NLAT, LON), ((0, 8),), -0.4, 0.0), -0.3, 0.3),
        "observed_cells": place_ends(jax.random.randint(key_list[5], (TIMES, N_LAT, NOBS), 0, ROWS * LON), jax.random.fold_in(key_list[5], 1), 0, (ROWS * LON) - 1).astype(jnp.int32),
        "observed_values": centred(key_list[6], (TIMES, N_LAT, NOBS), 1.0, 6.0, ((0, 4), (1, 8)), jnp.float32),
        "observed_weights": jnp.clip(jnp.exp(math.log(2.0) - 2.3025851 * jax.random.uniform(key_list[7], (TIMES, N_LAT, NOBS), jnp.float32) ** level_of(key_list[7], (TIMES, N_LAT, NOBS), ((0, 4), (1, 8)), -0.2, 0.2)), 0.2, 2.0),
        "fresh_cells": place_ends(jax.random.randint(key_list[8], (HALF, N_LAT, NOBS), 0, ROWS * LON), jax.random.fold_in(key_list[8], 1), 0, (ROWS * LON) - 1).astype(jnp.int32),
        "fresh_values": centred(key_list[9], (HALF, N_LAT, NOBS), 1.0, 6.0, ((1, 8),), jnp.float32),
        "fresh_weights": jnp.clip(jnp.exp(math.log(2.0) - 2.3025851 * jax.random.uniform(key_list[10], (HALF, N_LAT, NOBS), jnp.float32) ** level_of(key_list[10], (HALF, N_LAT, NOBS), ((1, 8),), -0.2, 0.2)), 0.2, 2.0),
    }


penalty_weight = 1.0
step_size = 0.15


def pad_rows(field):
    widths = [(0, 0)] * (field.ndim - 2) + [(1, 1), (0, 0)]
    padded = jnp.pad(field, widths)
    return padded[..., 2:, :], padded[..., :-2, :]


def substep_forward(field, diffusivity, zonal_speed, meridional_speed):
    north_cells, south_cells = pad_rows(field)
    east_cells = jnp.roll(field, -1, axis=-1)
    west_cells = jnp.roll(field, 1, axis=-1)
    return (field + diffusivity * (north_cells + south_cells + east_cells + west_cells - 4.0 * field)
            - 0.5 * zonal_speed * (east_cells - west_cells) - 0.5 * meridional_speed * (north_cells - south_cells))


def substep_adjoint(field, diffusivity, zonal_speed, meridional_speed):
    spread = diffusivity * field
    carried = 0.5 * zonal_speed * field
    lifted = 0.5 * meridional_speed * field
    spread_north, spread_south = pad_rows(spread)
    lifted_north, lifted_south = pad_rows(lifted)
    return (field + spread_north + spread_south + jnp.roll(spread, -1, axis=-1) + jnp.roll(spread, 1, axis=-1)
            - 4.0 * spread - jnp.roll(carried, 1, axis=-1) + jnp.roll(carried, -1, axis=-1)
            - lifted_south + lifted_north)


def reference(states, multipliers, diffusivity, zonal_speed, meridional_speed,
              observed_cells, observed_values, observed_weights, fresh_cells, fresh_values, fresh_weights):
    def forward(field):
        for substep in range(3):
            field = substep_forward(field, diffusivity, zonal_speed, meridional_speed)
        return field

    def backward(field):
        for substep in range(3):
            field = substep_adjoint(field, diffusivity, zonal_speed, meridional_speed)
        return field

    time_index = jnp.arange(TIMES, dtype=jnp.int32)[:, None, None]
    band_index = jnp.arange(N_LAT, dtype=jnp.int32)[None, :, None]

    def sweep(field, lagrange, prior, cells, values, weights):
        if prior is None:
            head = field[:1]
        else:
            head = prior[None]
        predicted = jnp.concatenate([head, forward(field[:-1])], axis=0)
        jumps = field - predicted
        flat = field.reshape(TIMES, N_LAT, ROWS * LON)
        misfit = weights * (jnp.take_along_axis(flat, cells, axis=2) - values)
        pulled_back = jnp.zeros_like(flat).at[time_index, band_index, cells].add(misfit).reshape(field.shape)
        pulled = lagrange + penalty_weight * jumps
        following = jnp.concatenate([pulled[1:], jnp.zeros_like(pulled[:1])], axis=0)
        gradient = pulled_back + pulled - backward(following)
        return field - step_size * gradient, lagrange + penalty_weight * jumps

    field, lagrange = states, multipliers
    cells, values, weights = observed_cells, observed_values, observed_weights
    for repeat in range(SWEEPS):
        field, lagrange = sweep(field, lagrange, None, cells, values, weights)
    next_prior = forward(field[HALF - 1])
    tail = jnp.broadcast_to(field[-1:], (HALF, NLAT, LON))
    field = jnp.concatenate([field[HALF:], tail], axis=0)
    lagrange = jnp.concatenate([lagrange[HALF:], jnp.zeros_like(lagrange[:HALF])], axis=0)
    cells = jnp.concatenate([cells[HALF:], fresh_cells], axis=0)
    values = jnp.concatenate([values[HALF:], fresh_values], axis=0)
    weights = jnp.concatenate([weights[HALF:], fresh_weights], axis=0)
    for repeat in range(SWEEPS):
        field, lagrange = sweep(field, lagrange, next_prior, cells, values, weights)
    return field, lagrange
```

```python
import functools

import jax
import jax.numpy as jnp
from jax import lax
from jax.experimental import pallas as pl
from jax.experimental.pallas import tpu as pltpu
from jax.sharding import PartitionSpec as P

penalty_weight = 1.0
step_size = 0.15

SUB = 8
MARGIN = 12
LROWS = 9
DROWS = 6
LANES = 128
STEPS = 2
PIECES = 3


def rolled(value, shift, axis):
    return pltpu.roll(value, shift % value.shape[axis], axis)


def sublane(shape):
    return lax.broadcasted_iota(jnp.int32, shape, len(shape) - 2)


def pack_rows(read, base, pairs, offset, write, at):
    for pair in range(pairs):
        first = read(base + 2 * pair)
        second = rolled(read(base + 2 * pair + 1), 4, 0)
        sub = sublane(first.shape)
        write(at + pair, jnp.where((sub >= offset) & (sub < offset + 4), first, second))


def eastward(value):
    half = value.shape[-1] // 2
    axis = value.ndim - 1
    return jnp.concatenate([value[..., half:], rolled(value[..., :half], -1, axis)], axis=axis)


def westward(value):
    half = value.shape[-1] // 2
    axis = value.ndim - 1
    return jnp.concatenate([rolled(value[..., half:], 1, axis), value[..., :half]], axis=axis)


def reordered(value, back=False):
    columns = value.shape[-1]
    natural = lax.broadcasted_iota(jnp.int32, (columns, columns), 1 if back else 0)
    parted = lax.broadcasted_iota(jnp.int32, (columns, columns), 0 if back else 1)
    target = (natural >> 1) + (natural & 1) * (columns // 2)
    moves = jnp.where(target == parted, 1.0, 0.0).astype(jnp.bfloat16)
    total = None
    for piece in reversed(split(value, 3)):
        part = jnp.dot(piece.astype(jnp.bfloat16), moves, preferred_element_type=jnp.float32)
        total = part if total is None else total + part
    return total


def interleave(lines_ref, slot, value):
    rows, columns = value.shape
    for part in range(columns // LANES):
        lines_ref[part, pl.ds(slot, rows, stride=SUB), :] = value[:, part * LANES : (part + 1) * LANES]


def copy_lines(lines_ref, dest_ref):
    rows = dest_ref.shape[0]
    for part in range(lines_ref.shape[0]):
        dest_ref[:, :, part * LANES : (part + 1) * LANES] = lines_ref[part].reshape(rows, SUB, LANES)


def prep_kernel(
    x_ref, l_ref, d_ref, z_ref, m_ref, cells_ref, values_ref, weights_ref,
    xa_ref, la_ref, coef_ref, tn_ref, lines_ref,
):
    slots, rows, columns = x_ref.shape
    for ref, dest in ((x_ref, xa_ref), (l_ref, la_ref)):
        value = reordered(ref[...].reshape(slots * rows, columns))
        for slot in range(slots):
            interleave(lines_ref, slot, value[slot * rows : (slot + 1) * rows])
        copy_lines(lines_ref, dest)
    for kind, ref in enumerate((d_ref, z_ref, m_ref)):
        coef_ref[kind] = reordered(ref[...])
    half = rows // 2

    def pair(step, carry):
        for ref, at in ((xa_ref, 0), (la_ref, half)):
            first = ref[2 * step]
            second = rolled(ref[2 * step + 1], 4, 0)
            tn_ref[at + step] = jnp.where(sublane(first.shape) < 4, first, second)
        return carry

    lax.fori_loop(0, half, pair, 0, unroll=4)
    parts = cells_ref.shape[2] // columns
    for kind, ref in enumerate((cells_ref, values_ref, weights_ref)):
        for slot in range(slots):
            for part in range(parts):
                tn_ref[rows + kind * parts + part, slot : slot + 1, :] = ref[
                    slot, :, part * columns : (part + 1) * columns
                ].astype(jnp.float32)


def split(value, count=PIECES):
    pieces = []
    for _ in range(count):
        piece = value.astype(jnp.bfloat16).astype(jnp.float32)
        pieces.append(piece)
        value = value - piece
    return pieces


def scatter(observed, slots, w_ref, v_ref, w_lines, v_lines):
    rows, _, columns = w_ref.shape
    count = observed(0)[0].shape[1]
    row_ids = lax.broadcasted_iota(jnp.int32, (rows, count), 0)
    column_ids = lax.broadcasted_iota(jnp.int32, (columns, count), 0)
    for slot in range(slots):
        cells, values, weights = observed(slot)
        row_of = cells // columns if columns & (columns - 1) else cells >> (columns.bit_length() - 1)
        column_of = cells - row_of * columns
        column_of = (column_of >> 1) + (column_of & 1) * (columns // 2)
        in_row = row_ids == row_of
        left = jnp.concatenate(
            [
                jnp.where(in_row, piece, 0.0).astype(jnp.bfloat16)
                for piece in split(weights) + split(weights * values)
            ],
            axis=0,
        )
        right = jnp.where(column_ids == column_of, 1.0, 0.0).astype(jnp.bfloat16)
        sums = lax.dot_general(
            left, right, (((1,), (1,)), ((), ())), preferred_element_type=jnp.float32
        )
        for lines, at in ((w_lines, 0), (v_lines, PIECES)):
            total = sums[at * rows : (at + 1) * rows]
            for piece in range(1, PIECES):
                total = total + sums[(at + piece) * rows : (at + piece + 1) * rows]
            interleave(lines, slot, total)
    for slot in range(slots, SUB):
        for lines in (w_lines, v_lines):
            interleave(lines, slot, jnp.zeros((rows, columns), jnp.float32))
    copy_lines(w_lines, w_ref)
    copy_lines(v_lines, v_ref)


def edge_kernel(
    xa_ref, la_ref, coef_ref, cells_ref, values_ref, weights_ref,
    w_ref, v_ref, up_ref, dn_ref, du_ref, dd_ref, d_ref, w_lines, v_lines,
):
    rows, _, columns = xa_ref.shape

    def observed(slot):
        return (cells_ref[slot], values_ref[slot], weights_ref[slot])

    scatter(observed, SUB, w_ref, v_ref, w_lines, v_lines)

    for row in range(DROWS):
        for at, where_row in ((row, rows - DROWS + row), (DROWS + row, row)):
            d_ref[at] = w_ref[where_row] * xa_ref[where_row] - v_ref[where_row]
    for ref, diag, xs, ls, ds in (
        (up_ref, du_ref, rows - MARGIN, rows - LROWS, 0),
        (dn_ref, dd_ref, 0, 0, DROWS),
    ):
        ref[0:MARGIN] = xa_ref[xs : xs + MARGIN]
        ref[MARGIN : MARGIN + LROWS] = la_ref[ls : ls + LROWS]
        ref[MARGIN + LROWS : MARGIN + LROWS + DROWS] = d_ref[ds : ds + DROWS]
        base = MARGIN + LROWS + DROWS
        for kind in range(3):
            flat = coef_ref[kind, xs : xs + MARGIN, :]
            for row in range(MARGIN):
                at = kind * MARGIN + row
                ref[base + at // SUB, at % SUB : at % SUB + 1, :] = flat[row : row + 1]
        for at in range(3 * MARGIN, (ref.shape[0] - base) * SUB):
            ref[base + at // SUB, at % SUB : at % SUB + 1, :] = jnp.zeros((1, columns), jnp.float32)

        def write(at, value, diag=diag):
            diag[at] = value

        lfirst = ls - (LROWS % 2) if ls else 0
        pack_rows(lambda row: xa_ref[row], xs, MARGIN // 2, 0, write, 0)
        pack_rows(lambda row: la_ref[row], lfirst, (LROWS + 1) // 2, 0, write, MARGIN // 2)
        pack_rows(lambda row: d_ref[row], ds, DROWS // 2, 0, write, MARGIN // 2 + (LROWS + 1) // 2)


def next_kernel(
    flag_ref, tn_ref, cells_ref, values_ref, weights_ref, w_ref, v_ref, lists_ref, w_lines, v_lines
):
    last = flag_ref[1] == 1
    rows = w_ref.shape[0]
    pltpu.sync_copy(tn_ref.at[rows : rows + lists_ref.shape[0]], lists_ref)
    parts = lists_ref.shape[0] // 3
    fresh_slots = cells_ref.shape[0]

    def observed(slot):
        out = []
        for kind, ref in enumerate((cells_ref, values_ref, weights_ref)):
            moved = jnp.concatenate(
                [lists_ref[kind * parts + part, slot : slot + 1, :] for part in range(parts)], axis=1
            )
            moved = moved.astype(ref.dtype)
            if slot < fresh_slots:
                moved = jnp.where(last, ref[slot], moved)
            elif kind == 2:
                moved = jnp.where(last, 0.0, moved)
            out.append(moved)
        return out

    scatter(observed, fresh_slots + 1, w_ref, v_ref, w_lines, v_lines)


def sweep_kernel(phase, *refs):
    if phase == 1:
        (flag_ref, xa_ref, la_ref, tn_ref, lo_ref, hi_ref, dlo_ref, dhi_ref, wa_ref, va_ref, wb_ref,
         vb_ref, coef_ref, *refs) = refs
        clo_ref, chi_ref = lo_ref, hi_ref
        (xa2_ref, la2_ref, xb2_ref, lb2_ref, tn2_ref, up_ref, dn_ref, du_ref, dd_ref, *refs) = refs
    else:
        (flag_ref, xa_ref, la_ref, xb_ref, lb_ref, tn_ref, lo_ref, hi_ref, dlo_ref, dhi_ref, wa_ref,
         va_ref, wb_ref, vb_ref, coef_ref, clo_ref, chi_ref, *refs) = refs
        (xout_ref, lout_ref, *refs) = refs
    xs_ref, ls_ref, ws_ref, vs_ref, p_ref, q_ref, flat_ref, cf_ref, lines_ref = refs
    rows, _, columns = xa_ref.shape
    first = flag_ref[0] == 1
    last = flag_ref[1] == 1
    top = MARGIN + rows
    half = rows // 2
    sub = sublane((SUB, columns))

    packed_coef = clo_ref.shape[0] - -(-3 * MARGIN // SUB)
    for kind in range(3):
        flat_ref[kind, MARGIN:top, :] = coef_ref[kind]
        for row in range(MARGIN):
            at = kind * MARGIN + row
            for base, ref in ((0, clo_ref), (top, chi_ref)):
                flat_ref[kind, base + row : base + row + 1, :] = ref[
                    packed_coef + at // SUB, at % SUB : at % SUB + 1, :
                ]
    total = rows + 2 * MARGIN
    diff = flat_ref[0, 0:total, :]
    zonal = 0.5 * flat_ref[1, 0:total, :]
    merid = 0.5 * flat_ref[2, 0:total, :]
    row_global = flag_ref[2] * rows - MARGIN + lax.broadcasted_iota(jnp.int32, diff.shape, 0)
    inside = (row_global >= 0) & (row_global < flag_ref[3] * rows)
    south = diff + merid
    north = diff - merid
    east = diff - zonal
    west = diff + zonal
    planes = (
        1.0 - 4.0 * diff,
        north,
        south,
        east,
        west,
        jnp.where(inside, rolled(south, -1, 0), 0.0),
        jnp.where(inside, rolled(north, 1, 0), 0.0),
        eastward(west),
        westward(east),
    )
    for index, plane in enumerate(planes):
        flat_ref[3 + index, 0:total, :] = plane

    def widen(step, carry):
        start = pl.multiple_of(step * 8, 8)
        for index in range(9):
            block = flat_ref[3 + index, pl.ds(start, 8), :]
            for row in range(8):
                cf_ref[index, start + row] = jnp.broadcast_to(block[row : row + 1], (SUB, columns))
        return carry

    lax.fori_loop(0, total // 8, widen, 0)

    xs_ref[MARGIN:top, 0] = xa_ref[...]
    ls_ref[MARGIN:top, 0] = la_ref[...]
    ws_ref[MARGIN:top, 0] = wa_ref[...]
    vs_ref[MARGIN:top, 0] = va_ref[...]
    ws_ref[MARGIN:top, 1] = wb_ref[...]
    vs_ref[MARGIN:top, 1] = vb_ref[...]
    zero = jnp.zeros((DROWS, 2, SUB, columns), jnp.float32)
    ws_ref[MARGIN - DROWS : MARGIN] = zero
    ws_ref[top : top + DROWS] = zero
    low, high = MARGIN + LROWS, MARGIN + LROWS + DROWS
    for ref, xat, lat_at, dat in (
        (lo_ref, 0, MARGIN - LROWS, MARGIN - DROWS),
        (hi_ref, top, top, top),
    ):
        xs_ref[xat : xat + MARGIN, 0] = ref[0:MARGIN]
        ls_ref[lat_at : lat_at + LROWS, 0] = ref[MARGIN:low]
        vs_ref[dat : dat + DROWS, 0] = -ref[low:high]

    def slot7(value):
        return jnp.broadcast_to(value[SUB - 1 : SUB], value.shape)

    def place(kind, at, pair, source, own, spare):
        dest = {"x": xs_ref, "l": ls_ref, "d": vs_ref}[kind]
        for odd, value in ((0, source), (1, rolled(source, 4, 0))):
            row = at + 2 * pair + odd
            if phase == 2:
                if kind == "d":
                    other = spare if odd == 0 else rolled(spare, 4, 0)
                    value = jnp.where(last, other, value)
                value = jnp.where(sub < 2, own(2 * pair + odd), value)
                if kind == "x":
                    value = jnp.where(last, slot7(xs_ref[row, 0]), value)
                elif kind == "l":
                    value = jnp.where(last, 0.0, value)
            dest[row, 1] = -value if kind == "d" else value

    own_x = (lambda row: xb_ref[row]) if phase == 2 else None
    own_l = (lambda row: lb_ref[row]) if phase == 2 else None

    def interior(step, carry):
        place("x", MARGIN, step, tn_ref[step], own_x, None)
        place("l", MARGIN, step, tn_ref[half + step], own_l, None)
        return carry

    lax.fori_loop(0, half, interior, 0, unroll=2)
    lpairs = (LROWS + 1) // 2
    dbase = MARGIN // 2 + lpairs
    for ref, diag, at, lat_at, lskip, dat in (
        (lo_ref, dlo_ref, 0, MARGIN - 2 * lpairs, 1, MARGIN - DROWS),
        (hi_ref, dhi_ref, top, top, 0, top),
    ):
        for pair in range(MARGIN // 2):
            place("x", at, pair, diag[pair], lambda row, ref=ref: ref[row], None)
        for pair in range(lpairs):
            place(
                "l", lat_at, pair, diag[MARGIN // 2 + pair],
                lambda row, ref=ref, lskip=lskip: ref[
                    MARGIN + min(max(row - lskip, 0), LROWS - 1)
                ],
                None,
            )
        for pair in range(DROWS // 2):
            spare = ref[high + pair] if phase == 2 else None
            place(
                "d", dat, pair, diag[dbase + pair], lambda row, ref=ref: ref[low + row], spare
            )

    keep = jnp.logical_not(last)
    if phase == 2:
        keep = keep | (sub < 4)
    else:
        keep = keep & (sub < SUB)
    frozen = first & (sub < 4)

    def stencil(src, adjoint, reach, finish):
        base = 5 if adjoint else 1
        start = MARGIN - reach
        block = pl.cdiv(rows + 2 * reach, STEPS)

        def step(index, carry):
            row0 = start + index * block
            for row in range(block):
                at = row0 + row
                coef = [cf_ref[k, at] for k in (0, base, base + 1, base + 2, base + 3)]
                out = []
                for tile in range(2):
                    value = src[at, tile]
                    out.append(
                        coef[0] * value
                        + coef[1] * src[at + 1, tile]
                        + coef[2] * src[at - 1, tile]
                        + coef[3] * eastward(value)
                        + coef[4] * westward(value)
                    )
                finish(at, out)
            return carry

        lax.fori_loop(0, STEPS, step, 0)

    def store(dest):
        def finish(at, out):
            dest[at, 0] = out[0]
            dest[at, 1] = out[1]

        return finish

    def forward_end(at, out):
        ahead_a = rolled(out[0], 1, 0)
        ahead_b = rolled(out[1], 1, 0)
        ahead_b = jnp.where(sub == 0, ahead_a, ahead_b)
        jump_a = jnp.where(sub == 0, 0.0, xs_ref[at, 0] - ahead_a)
        jump_b = xs_ref[at, 1] - ahead_b
        ls_ref[at, 0] = ls_ref[at, 0] + jump_a
        ls_ref[at, 1] = jnp.where(keep, ls_ref[at, 1] + jump_b, 0.0)

    def backward_end(at, out):
        back_a = rolled(out[0], -1, 0)
        back_b = rolled(out[1], -1, 0)
        back_a = jnp.where(sub == SUB - 1, back_b, back_a)
        for tile, after in ((0, back_a), (1, back_b)):
            value = xs_ref[at, tile]
            gradient = ws_ref[at, tile] * value - vs_ref[at, tile] + ls_ref[at, tile] - after
            new = value - step_size * gradient
            if phase == 2 and tile == 0:
                new = jnp.where(frozen, value, new)
            xs_ref[at, tile] = new

    for reach in (MARGIN, MARGIN // 2):
        stencil(xs_ref, False, reach - 1, store(p_ref))
        stencil(p_ref, False, reach - 2, store(q_ref))
        stencil(q_ref, False, reach - 3, forward_end)
        stencil(ls_ref, True, reach - 4, store(p_ref))
        stencil(p_ref, True, reach - 5, store(q_ref))
        stencil(q_ref, True, reach - 6, backward_end)

    if phase == 2:
        parts = columns // LANES
        for ref, dest in ((xs_ref, xout_ref), (ls_ref, lout_ref)):

            def gather(step, carry, ref=ref):
                value = jnp.where(
                    sub < 4,
                    rolled(ref[MARGIN + step, 0], 4, 0),
                    rolled(ref[MARGIN + step, 1], 4, 0),
                )
                for part in range(parts):
                    lines_ref[part, pl.ds(pl.multiple_of(step * SUB, SUB), SUB), :] = value[
                        :, part * LANES : (part + 1) * LANES
                    ]
                return carry

            lax.fori_loop(0, rows, gather, 0, unroll=4)
            value = jnp.concatenate(
                [
                    jnp.concatenate(
                        [lines_ref[part, pl.ds(slot, rows, stride=SUB), :] for part in range(parts)],
                        axis=1,
                    )
                    for slot in range(SUB)
                ],
                axis=0,
            )
            dest[...] = reordered(value, back=True).reshape(dest.shape)
        return

    def fix(step, carry):
        at = MARGIN + step
        value = xs_ref[at, 1]
        xs_ref[at, 1] = jnp.where(last, slot7(xs_ref[at, 0]), value)
        return carry

    lax.fori_loop(0, rows, fix, 0, unroll=4)
    xa2_ref[...] = xs_ref[MARGIN:top, 0]
    la2_ref[...] = ls_ref[MARGIN:top, 0]
    xb2_ref[...] = xs_ref[MARGIN:top, 1]
    lb2_ref[...] = ls_ref[MARGIN:top, 1]

    def packed(ref, at, tile):
        second = rolled(ref[at + 1, tile], 4, 0)
        return jnp.where((sub >= 2) & (sub < 6), ref[at, tile], second)

    def send(step, carry):
        tn2_ref[step] = packed(xs_ref, MARGIN + 2 * step, 0)
        tn2_ref[half + step] = packed(ls_ref, MARGIN + 2 * step, 0)
        return carry

    lax.fori_loop(0, half, send, 0, unroll=2)

    def owned(ref, at):
        return jnp.where(sub < 2, ref[at, 1], ref[at, 0])

    for ref, diag, xat, lat_at, lfirst, dat in (
        (up_ref, du_ref, top - MARGIN, top - LROWS, top - 2 * lpairs, top - DROWS),
        (dn_ref, dd_ref, MARGIN, MARGIN, MARGIN, MARGIN),
    ):
        for row in range(DROWS):
            at = dat + row
            for tile in range(2):
                p_ref[at, tile] = ws_ref[at, tile] * xs_ref[at, tile] - vs_ref[at, tile]
        for row in range(MARGIN):
            ref[row] = owned(xs_ref, xat + row)
        for row in range(LROWS):
            ref[MARGIN + row] = owned(ls_ref, lat_at + row)
        for row in range(DROWS):
            ref[low + row] = owned(p_ref, dat + row)
        for pair in range(DROWS // 2):
            ref[high + pair] = packed(p_ref, dat + 2 * pair, 1)
        for pair in range(MARGIN // 2):
            diag[pair] = packed(xs_ref, xat + 2 * pair, 0)
        for pair in range(lpairs):
            diag[MARGIN // 2 + pair] = packed(ls_ref, lfirst + 2 * pair, 0)
        for pair in range(DROWS // 2):
            diag[dbase + pair] = packed(p_ref, dat + 2 * pair, 0)


def body(
    states,
    multipliers,
    diffusivity,
    zonal_speed,
    meridional_speed,
    observed_cells,
    observed_values,
    observed_weights,
    fresh_cells,
    fresh_values,
    fresh_weights,
):
    slots, rows, columns = states.shape
    half = fresh_cells.shape[0]
    tm_count, lat_count = lax.axis_size("tm"), lax.axis_size("lat")
    tm_index, lat_index = lax.axis_index("tm"), lax.axis_index("lat")
    flags = jnp.stack(
        [
            (tm_index == 0).astype(jnp.int32),
            (tm_index == tm_count - 1).astype(jnp.int32),
            lat_index.astype(jnp.int32),
            jnp.int32(lat_count),
        ]
    )

    def send(value, tm_step, lat_step):
        pairs = []
        for t in range(tm_count):
            for b in range(lat_count):
                to_t, to_b = t + tm_step, b + lat_step
                if 0 <= to_t < tm_count and 0 <= to_b < lat_count:
                    pairs.append((t * lat_count + b, to_t * lat_count + to_b))
        return lax.ppermute(value, ("tm", "lat"), pairs)

    smem = pl.BlockSpec(memory_space=pltpu.SMEM)
    vmem = pl.BlockSpec(memory_space=pltpu.VMEM)

    def call(kernel, outs, args, scratch=(), flagged=False, hbm=()):
        specs = [vmem] * len(args)
        for index in hbm:
            specs[index] = pl.BlockSpec(memory_space=pl.ANY)
        if flagged:
            args, specs = (flags, *args), [smem] + specs
        return pl.pallas_call(
            kernel,
            out_shape=[jax.ShapeDtypeStruct(shape, jnp.float32) for shape in outs],
            in_specs=specs,
            out_specs=[vmem] * len(outs),
            scratch_shapes=list(scratch),
        )(*args)

    tile = (SUB, columns)
    lines = pltpu.VMEM((columns // LANES, rows * SUB, LANES), jnp.float32)
    field = (rows, *tile)
    count = observed_cells.shape[-1]
    lists = 3 * (count // columns)
    diag = (MARGIN // 2 + (LROWS + 1) // 2 + DROWS // 2, *tile)
    edge = MARGIN + LROWS + DROWS
    coef_rows = -(-3 * MARGIN // SUB)

    obs = (observed_cells, observed_values, observed_weights)

    xa, la, coef, tn = call(
        prep_kernel,
        (field, field, (3, rows, columns), (rows + lists, *tile)),
        (states, multipliers, diffusivity, zonal_speed, meridional_speed, *obs),
        (lines,),
    )
    tn = send(tn, -1, 0)
    wa, va, up, dn, du, dd = call(
        edge_kernel,
        (field, field, (edge + coef_rows, *tile), (edge + coef_rows, *tile), diag, diag),
        (xa, la, coef, *obs),
        (pltpu.VMEM((2 * DROWS, *tile), jnp.float32), lines, lines),
    )
    lo = send(up, 0, 1)
    hi = send(dn, 0, -1)
    dlo = send(du, -1, 1)
    dhi = send(dd, -1, -1)

    wb, vb = call(
        next_kernel,
        (field, field),
        (tn, fresh_cells, fresh_values, fresh_weights),
        (pltpu.VMEM((lists, *tile), jnp.float32), lines, lines),
        flagged=True,
        hbm=(0,),
    )
    obs = (wa, va, wb, vb)
    coef_halos = (lo, hi)

    reach = rows + 2 * MARGIN + 8
    scratch = (
        [pltpu.VMEM((reach, 2, *tile), jnp.float32)] * 6
        + [pltpu.VMEM((12, reach, columns), jnp.float32)]
        + [pltpu.VMEM((9, reach, *tile), jnp.float32), lines]
    )
    edge2 = (edge + DROWS // 2, *tile)
    xa2, la2, xb2, lb2, tn2, up, dn, du, dd = call(
        functools.partial(sweep_kernel, 1),
        (field, field, field, field, field, edge2, edge2, diag, diag),
        (xa, la, tn, lo, hi, dlo, dhi, *obs, coef),
        scratch,
        flagged=True,
    )
    tn2 = send(tn2, -1, 0)
    lo = send(up, 0, 1)
    hi = send(dn, 0, -1)
    dlo = send(du, -1, 1)
    dhi = send(dd, -1, -1)
    analysis, lagrange = call(
        functools.partial(sweep_kernel, 2),
        (states.shape, states.shape),
        (xa2, la2, xb2, lb2, tn2, lo, hi, dlo, dhi, *obs, coef, *coef_halos),
        scratch,
        flagged=True,
    )
    return (analysis, lagrange)


def solution(mesh):
    in_specs = (
        P("tm", "lat", None),
        P("tm", "lat", None),
        P("lat", None),
        P("lat", None),
        P("lat", None),
        P("tm", "lat", None),
        P("tm", "lat", None),
        P("tm", "lat", None),
        P(None, "lat", None),
        P(None, "lat", None),
        P(None, "lat", None),
    )
    out_specs = (P("tm", "lat", None), P("tm", "lat", None))
    return jax.shard_map(body, mesh=mesh, in_specs=in_specs, out_specs=out_specs, check_vma=False)
```

```python
import jax
import jax.numpy as jnp
from jax import lax
from jax.experimental import pallas as pl
from jax.experimental.pallas import tpu as pltpu
from jax.sharding import PartitionSpec as P

penalty_weight = 1.0
step_size = 0.15

SUB = 8
MARGIN = 12
LROWS = 9
DROWS = 6
EDGE = MARGIN + LROWS + DROWS
PAIRS = MARGIN // 2 + (LROWS + 1) // 2 + DROWS // 2
STRIP = 3 * MARGIN
LANES = 128
PIECES = 3


def rolled(value, shift, axis):
    return pltpu.roll(value, shift % value.shape[axis], axis)


def sublane(shape):
    return lax.broadcasted_iota(jnp.int32, shape, len(shape) - 2)


def two_rows(first, second):
    sub = sublane(first.shape)
    return jnp.where((sub >= 2) & (sub < 6), first, rolled(second, 4, 0))


def eastward(value):
    half = value.shape[-1] // 2
    axis = value.ndim - 1
    return jnp.concatenate([value[..., half:], rolled(value[..., :half], -1, axis)], axis=axis)


def westward(value):
    half = value.shape[-1] // 2
    axis = value.ndim - 1
    return jnp.concatenate([rolled(value[..., half:], 1, axis), value[..., :half]], axis=axis)


def reordered(value, back=False):
    columns = value.shape[-1]
    natural = lax.broadcasted_iota(jnp.int32, (columns, columns), 1 if back else 0)
    parted = lax.broadcasted_iota(jnp.int32, (columns, columns), 0 if back else 1)
    target = (natural >> 1) + (natural & 1) * (columns // 2)
    moves = jnp.where(target == parted, 1.0, 0.0).astype(jnp.bfloat16)
    total = None
    for piece in reversed(split(value, 3)):
        part = jnp.dot(piece.astype(jnp.bfloat16), moves, preferred_element_type=jnp.float32)
        total = part if total is None else total + part
    return total


def interleave(lines_ref, slot, value):
    rows, columns = value.shape
    for part in range(columns // LANES):
        lines_ref[part, pl.ds(slot, rows, stride=SUB), :] = value[:, part * LANES : (part + 1) * LANES]


def copy_lines(lines_ref, dest_ref):
    rows = dest_ref.shape[0]
    for part in range(lines_ref.shape[0]):
        dest_ref[:, :, part * LANES : (part + 1) * LANES] = lines_ref[part].reshape(rows, SUB, LANES)


def prep_kernel(
    x_ref, l_ref, d_ref, z_ref, m_ref, cells_ref, values_ref, weights_ref,
    tn_ref, coef_ref, lines_ref,
):
    slots, rows, columns = x_ref.shape
    for ref, dest in ((x_ref, tn_ref.at[0:rows]), (l_ref, tn_ref.at[rows : 2 * rows])):
        value = reordered(ref[...].reshape(slots * rows, columns))
        for slot in range(slots):
            interleave(lines_ref, slot, value[slot * rows : (slot + 1) * rows])
        copy_lines(lines_ref, dest)
    for kind, ref in enumerate((d_ref, z_ref, m_ref)):
        coef_ref[kind] = reordered(ref[...])
    parts = cells_ref.shape[2] // columns
    for kind, ref in enumerate((cells_ref, values_ref, weights_ref)):
        for slot in range(slots):
            for part in range(parts):
                tn_ref[2 * rows + kind * parts + part, slot : slot + 1, :] = ref[
                    slot, :, part * columns : (part + 1) * columns
                ].astype(jnp.float32)


def split(value, count=PIECES):
    pieces = []
    for _ in range(count):
        piece = value.astype(jnp.bfloat16).astype(jnp.float32)
        pieces.append(piece)
        value = value - piece
    return pieces


def scatter(observed, slots, row_ids, columns, w_lines, v_lines):
    rows, count = row_ids.shape
    column_ids = lax.broadcasted_iota(jnp.int32, (columns, count), 0)
    for slot in range(slots):
        cells, values, weights = observed(slot)
        row_of = cells // columns if columns & (columns - 1) else cells >> (columns.bit_length() - 1)
        column_of = cells - row_of * columns
        column_of = (column_of >> 1) + (column_of & 1) * (columns // 2)
        in_row = row_ids == row_of
        left = jnp.concatenate(
            [
                jnp.where(in_row, piece, 0.0).astype(jnp.bfloat16)
                for piece in split(weights) + split(weights * values)
            ],
            axis=0,
        )
        right = jnp.where(column_ids == column_of, 1.0, 0.0).astype(jnp.bfloat16)
        sums = lax.dot_general(
            left, right, (((1,), (1,)), ((), ())), preferred_element_type=jnp.float32
        )
        for lines, at in ((w_lines, 0), (v_lines, PIECES)):
            total = sums[at * rows : (at + 1) * rows]
            for piece in range(1, PIECES):
                total = total + sums[(at + piece) * rows : (at + piece + 1) * rows]
            interleave(lines, slot, total)
    for slot in range(slots, SUB):
        for lines in (w_lines, v_lines):
            interleave(lines, slot, jnp.zeros((rows, columns), jnp.float32))


def edge_kernel(
    xl_ref, coef_ref, cells_ref, values_ref, weights_ref,
    up_ref, dn_ref, du_ref, dd_ref, w_ref, v_ref, w_lines, v_lines,
):
    rows, columns = coef_ref.shape[1:]

    def observed(slot):
        return (cells_ref[slot], values_ref[slot], weights_ref[slot])

    lines = lax.broadcasted_iota(jnp.int32, (w_ref.shape[0], cells_ref.shape[2]), 0)
    row_ids = jnp.where(lines < DROWS, lines, lines + rows - 2 * DROWS)
    scatter(observed, SUB, row_ids, columns, w_lines, v_lines)
    copy_lines(w_lines, w_ref)
    copy_lines(v_lines, v_ref)
    for ref, diag, xs, ls, ds, ws in (
        (up_ref, du_ref, rows - MARGIN, rows - LROWS, rows - DROWS, DROWS),
        (dn_ref, dd_ref, 0, 0, 0, 0),
    ):
        for dest in (ref, diag):
            dest[0:MARGIN] = xl_ref[xs : xs + MARGIN]
            dest[MARGIN : MARGIN + LROWS] = xl_ref[rows + ls : rows + ls + LROWS]
            dest[MARGIN + LROWS : EDGE] = (
                w_ref[ws : ws + DROWS] * xl_ref[ds : ds + DROWS] - v_ref[ws : ws + DROWS]
            )
        for kind in range(3):
            flat = coef_ref[kind, xs : xs + MARGIN, :]
            for row in range(MARGIN):
                at = kind * MARGIN + row
                ref[EDGE + at // SUB, at % SUB : at % SUB + 1, :] = flat[row : row + 1]
        for at in range(3 * MARGIN, (ref.shape[0] - EDGE) * SUB):
            ref[EDGE + at // SUB, at % SUB : at % SUB + 1, :] = jnp.zeros((1, columns), jnp.float32)


def observation_kernel(
    tn_ref, cells_ref, values_ref, weights_ref, *refs
):
    fresh, (wa_ref, va_ref, wb_ref, vb_ref, lists_ref, w_lines, v_lines) = refs[:3], refs[3:]
    last = lax.axis_index("tm") == lax.axis_size("tm") - 1
    rows, _, columns = wa_ref.shape
    pltpu.sync_copy(tn_ref.at[2 * rows : 2 * rows + lists_ref.shape[0]], lists_ref)
    parts = lists_ref.shape[0] // 3
    fresh_slots = fresh[0].shape[0]
    row_ids = lax.broadcasted_iota(jnp.int32, (rows, cells_ref.shape[2]), 0)

    def own(slot):
        return (cells_ref[slot], values_ref[slot], weights_ref[slot])

    def following(slot):
        out = []
        for kind, ref in enumerate(fresh):
            moved = jnp.concatenate(
                [lists_ref[kind * parts + part, slot : slot + 1, :] for part in range(parts)], axis=1
            )
            moved = moved.astype(ref.dtype)
            if slot < fresh_slots:
                moved = jnp.where(last, ref[slot], moved)
            elif kind == 2:
                moved = jnp.where(last, 0.0, moved)
            out.append(moved)
        return out

    scatter(own, SUB, row_ids, columns, w_lines, v_lines)
    copy_lines(w_lines, wa_ref)
    copy_lines(v_lines, va_ref)
    scatter(following, SUB - 1, row_ids, columns, w_lines, v_lines)
    copy_lines(w_lines, wb_ref)
    copy_lines(v_lines, vb_ref)


def slot7(value):
    return jnp.broadcast_to(value[SUB - 1 : SUB], value.shape)


def widen_coefficients(flat_ref, cf_ref, total, row_of):
    rows_all = lax.axis_size("lat") * row_of[1]
    diff = flat_ref[0, 0:total, :]
    zonal = 0.5 * flat_ref[1, 0:total, :]
    merid = 0.5 * flat_ref[2, 0:total, :]
    row_global = lax.axis_index("lat") * row_of[1] + row_of[0](
        lax.broadcasted_iota(jnp.int32, diff.shape, 0)
    )
    inside = (row_global >= 0) & (row_global < rows_all)
    south = diff + merid
    north = diff - merid
    east = diff - zonal
    west = diff + zonal
    planes = (
        1.0 - 4.0 * diff,
        north,
        south,
        east,
        west,
        jnp.where(inside, rolled(south, -1, 0), 0.0),
        jnp.where(inside, rolled(north, 1, 0), 0.0),
        eastward(west),
        westward(east),
    )
    for index, plane in enumerate(planes):
        flat_ref[3 + index, 0:total, :] = plane

    def widen(step, carry):
        start = pl.multiple_of(step * SUB, SUB)
        for index in range(len(planes)):
            block = flat_ref[3 + index, pl.ds(start, SUB), :]
            for row in range(SUB):
                cf_ref[index, start + row] = jnp.broadcast_to(block[row : row + 1], block.shape)
        return carry

    lax.fori_loop(0, total // SUB, widen, 0)


def sweep(state, begin, stride, length, keep, frozen=None):
    xs_ref, ls_ref, ws_ref, vs_ref, p_ref, q_ref, cf_ref = state
    sub = sublane(xs_ref.shape[2:])

    def stencil(src, adjoint, depth, finish):
        base = 5 if adjoint else 1
        count = length - 2 * depth
        block = (count + 1) // 2
        offsets = list(range(count)) + list(range(stride, stride + count)) if stride else range(block)

        def step(index, carry):
            for row in offsets:
                at = begin + depth + index * block + row
                coef = [cf_ref[k, at] for k in (0, base, base + 1, base + 2, base + 3)]
                out = []
                for tile in range(2):
                    value = src[at, tile]
                    out.append(
                        coef[0] * value
                        + coef[1] * src[at + 1, tile]
                        + coef[2] * src[at - 1, tile]
                        + coef[3] * eastward(value)
                        + coef[4] * westward(value)
                    )
                finish(at, out)
            return carry

        if stride:
            step(0, 0)
        else:
            lax.fori_loop(0, 2, step, 0)

    def store(dest):
        def finish(at, out):
            dest[at, 0] = out[0]
            dest[at, 1] = out[1]

        return finish

    def forward_end(at, out):
        ahead_a = rolled(out[0], 1, 0)
        ahead_b = rolled(out[1], 1, 0)
        ahead_b = jnp.where(sub == 0, ahead_a, ahead_b)
        jump_a = jnp.where(sub == 0, 0.0, xs_ref[at, 0] - ahead_a)
        jump_b = xs_ref[at, 1] - ahead_b
        ls_ref[at, 0] = ls_ref[at, 0] + penalty_weight * jump_a
        ls_ref[at, 1] = jnp.where(keep, ls_ref[at, 1] + penalty_weight * jump_b, 0.0)

    def backward_end(at, out):
        back_a = rolled(out[0], -1, 0)
        back_b = rolled(out[1], -1, 0)
        back_a = jnp.where(sub == SUB - 1, back_b, back_a)
        for tile, after in ((0, back_a), (1, back_b)):
            value = xs_ref[at, tile]
            gradient = ws_ref[at, tile] * value - vs_ref[at, tile] + ls_ref[at, tile] - after
            new = value - step_size * gradient
            if frozen is not None and tile == 0:
                new = jnp.where(frozen, value, new)
            xs_ref[at, tile] = new

    stencil(xs_ref, False, 1, store(p_ref))
    stencil(p_ref, False, 2, store(q_ref))
    stencil(q_ref, False, 3, forward_end)
    stencil(ls_ref, True, 4, store(p_ref))
    stencil(p_ref, True, 5, store(q_ref))
    stencil(q_ref, True, 6, backward_end)


def time_ends():
    tm = lax.axis_index("tm")
    return tm == 0, tm == lax.axis_size("tm") - 1


def load_own(state, at, xl_ref, tn_ref, obs, first_row, count):
    xs_ref, ls_ref, ws_ref, vs_ref = state[:4]
    rows = obs[0].shape[0]
    for tile, ref in ((0, xl_ref), (1, tn_ref)):
        xs_ref[at : at + count, tile] = ref[first_row : first_row + count]
        ls_ref[at : at + count, tile] = ref[rows + first_row : rows + first_row + count]
        ws_ref[at : at + count, tile] = obs[2 * tile][first_row : first_row + count]
        vs_ref[at : at + count, tile] = obs[2 * tile + 1][first_row : first_row + count]


def outer_observations(state, at, rows_of):
    ws_ref, vs_ref = state[2:4]
    ws_ref[at : at + DROWS] = jnp.zeros((DROWS, *ws_ref.shape[1:]), jnp.float32)
    for row in range(DROWS):
        for tile in range(2):
            vs_ref[at + row, tile] = -rows_of(row, tile)


def strip_kernel(
    xl_ref, tn_ref, lo_ref, hi_ref, dlo_ref, dhi_ref, wa_ref, va_ref, wb_ref, vb_ref, coef_ref,
    x1_ref, l1_ref, x2_ref, l2_ref, up_ref, dn_ref, halo_ref, *state,
):
    state, flat_ref = state[:7], state[7]
    xs_ref, ls_ref, ws_ref, vs_ref, p_ref = state[:5]
    rows, _, columns = wa_ref.shape
    obs = (wa_ref, va_ref, wb_ref, vb_ref)
    _, last = time_ends()
    sub = sublane((SUB, columns))
    inner = STRIP - MARGIN
    total = 2 * STRIP
    for kind in range(3):
        for row in range(MARGIN):
            at = kind * MARGIN + row
            for base, ref in ((0, lo_ref), (MARGIN, hi_ref)):
                halo_ref[kind, base + row : base + row + 1, :] = ref[
                    EDGE + at // SUB, at % SUB : at % SUB + 1, :
                ]
        flat_ref[kind, 0:MARGIN, :] = halo_ref[kind, 0:MARGIN, :]
        flat_ref[kind, MARGIN:STRIP, :] = coef_ref[kind, 0:inner, :]
        flat_ref[kind, STRIP : STRIP + inner, :] = coef_ref[kind, rows - inner : rows, :]
        flat_ref[kind, STRIP + inner : total, :] = halo_ref[kind, MARGIN : 2 * MARGIN, :]
    widen_coefficients(
        flat_ref,
        state[6],
        total,
        (lambda at: jnp.where(at < STRIP, at - MARGIN, at - STRIP + rows - inner), rows),
    )
    load_own(state, MARGIN, xl_ref, tn_ref, obs, 0, MARGIN)
    load_own(state, STRIP + MARGIN, xl_ref, tn_ref, obs, rows - MARGIN, MARGIN)
    for refs, xat, lat_at, dat in (
        ((lo_ref, dlo_ref), 0, MARGIN - LROWS, MARGIN - DROWS),
        ((hi_ref, dhi_ref), STRIP + inner, STRIP + inner, STRIP + inner),
    ):
        for tile, ref in enumerate(refs):
            xs_ref[xat : xat + MARGIN, tile] = ref[0:MARGIN]
            ls_ref[lat_at : lat_at + LROWS, tile] = ref[MARGIN : MARGIN + LROWS]
        outer_observations(
            state, dat, lambda row, tile, refs=refs: refs[tile][MARGIN + LROWS + row]
        )
    keep = jnp.logical_not(last)
    sweep(state, 0, STRIP + MARGIN, 2 * MARGIN, keep)
    for dest, ref in ((xs_ref, x1_ref), (ls_ref, l1_ref)):
        count = ref.shape[0]
        dest[MARGIN + DROWS : 2 * MARGIN + DROWS] = ref[0:MARGIN]
        dest[STRIP + DROWS : STRIP + DROWS + MARGIN] = ref[count - MARGIN : count]
    sweep(state, DROWS, STRIP, 2 * MARGIN, keep)

    for ref, out, xat, lat_at, lpair, dat in (
        (dn_ref, 0, MARGIN, MARGIN, MARGIN, MARGIN),
        (
            up_ref,
            MARGIN,
            total - 2 * MARGIN,
            total - MARGIN - LROWS,
            total - MARGIN - 2 * ((LROWS + 1) // 2),
            total - MARGIN - DROWS,
        ),
    ):
        for row in range(MARGIN):
            at = xat + row
            xs_ref[at, 1] = jnp.where(last, slot7(xs_ref[at, 0]), xs_ref[at, 1])
        x2_ref[out : out + MARGIN] = xs_ref[xat : xat + MARGIN]
        l2_ref[out : out + MARGIN] = ls_ref[xat : xat + MARGIN]
        for row in range(DROWS):
            at = dat + row
            for tile in range(2):
                p_ref[at, tile] = ws_ref[at, tile] * xs_ref[at, tile] - vs_ref[at, tile]
        wide = narrow = 0
        for src, at, count, pair_at in (
            (xs_ref, xat, MARGIN, xat),
            (ls_ref, lat_at, LROWS, lpair),
            (p_ref, dat, DROWS, dat),
        ):
            for row in range(count):
                ref[wide + row] = jnp.where(sub < 2, src[at + row, 1], src[at + row, 0])
            wide += count
            for pair in range((count + 1) // 2):
                here = pair_at + 2 * pair
                ref[EDGE + narrow + pair] = two_rows(src[here, 1], src[here + 1, 1])
            narrow += (count + 1) // 2


def middle_kernel(
    xl_ref, tn_ref, wa_ref, va_ref, wb_ref, vb_ref, coef_ref, x1_ref, l1_ref, *state
):
    state, flat_ref = state[:7], state[7]
    xs_ref, ls_ref = state[:2]
    rows = wa_ref.shape[0]
    _, last = time_ends()
    for kind in range(3):
        flat_ref[kind, 0:rows, :] = coef_ref[kind]
    widen_coefficients(flat_ref, state[6], rows, (lambda at: at, rows))
    load_own(state, 0, xl_ref, tn_ref, (wa_ref, va_ref, wb_ref, vb_ref), 0, rows)
    sweep(state, 0, 0, rows, jnp.logical_not(last))
    x1_ref[...] = xs_ref[DROWS : rows - DROWS]
    l1_ref[...] = ls_ref[DROWS : rows - DROWS]


def inner_kernel(
    xstrip_ref, lstrip_ref, x1_ref, l1_ref, wa_ref, va_ref, wb_ref, vb_ref, coef_ref,
    x3_ref, l3_ref, *state,
):
    state, flat_ref = state[:7], state[7]
    xs_ref, ls_ref, ws_ref, vs_ref = state[:4]
    rows, _, columns = wa_ref.shape
    first, last = time_ends()
    sub = sublane((SUB, columns))
    for kind in range(3):
        flat_ref[kind, 0:rows, :] = coef_ref[kind]
    widen_coefficients(flat_ref, state[6], rows, (lambda at: at, rows))
    for tile, w, v in ((0, wa_ref, va_ref), (1, wb_ref, vb_ref)):
        ws_ref[0:rows, tile] = w[...]
        vs_ref[0:rows, tile] = v[...]
    xs_ref[DROWS : rows - DROWS] = x1_ref[...]
    ls_ref[DROWS : rows - DROWS] = l1_ref[...]
    sweep(state, DROWS, 0, rows - 2 * DROWS, jnp.logical_not(last))

    def fix(step, carry):
        at = MARGIN + step
        xs_ref[at, 1] = jnp.where(last, slot7(xs_ref[at, 0]), xs_ref[at, 1])
        return carry

    lax.fori_loop(0, rows - 2 * MARGIN, fix, 0, unroll=4)
    for dest, strip in ((xs_ref, xstrip_ref), (ls_ref, lstrip_ref)):
        dest[0:MARGIN] = strip[0:MARGIN]
        dest[rows - MARGIN : rows] = strip[MARGIN : 2 * MARGIN]
    sweep(state, 0, 0, rows, jnp.logical_not(last) | (sub < 4), first & (sub < 4))
    x3_ref[...] = xs_ref[DROWS : rows - DROWS]
    l3_ref[...] = ls_ref[DROWS : rows - DROWS]


def final_kernel(
    xstrip_ref, lstrip_ref, x3_ref, l3_ref, lo_ref, hi_ref, wa_ref, va_ref, wb_ref, vb_ref,
    coef_ref, halo_ref, xout_ref, lout_ref, *state,
):
    state, flat_ref, lines_ref = state[:7], state[7], state[8]
    xs_ref, ls_ref, ws_ref, vs_ref = state[:4]
    rows, _, columns = wa_ref.shape
    first, last = time_ends()
    top = MARGIN + rows
    sub = sublane((SUB, columns))
    for kind in range(3):
        flat_ref[kind, 0:MARGIN, :] = halo_ref[kind, 0:MARGIN, :]
        flat_ref[kind, MARGIN:top, :] = coef_ref[kind]
        flat_ref[kind, top : top + MARGIN, :] = halo_ref[kind, MARGIN : 2 * MARGIN, :]
    widen_coefficients(flat_ref, state[6], rows + 2 * MARGIN, (lambda at: at - MARGIN, rows))
    for dest, strip in ((xs_ref, xstrip_ref), (ls_ref, lstrip_ref)):
        dest[MARGIN : 2 * MARGIN] = strip[0:MARGIN]
        dest[top - MARGIN : top] = strip[MARGIN : 2 * MARGIN]
    for tile, w, v in ((0, wa_ref, va_ref), (1, wb_ref, vb_ref)):
        ws_ref[MARGIN:top, tile] = w[...]
        vs_ref[MARGIN:top, tile] = v[...]

    for ref, xat, lat_at, lskip, dat in (
        (lo_ref, 0, MARGIN - LROWS, LROWS % 2, MARGIN - DROWS),
        (hi_ref, top, top, 0, top),
    ):

        def outer(row, tile, wide, narrow, skip, ref=ref):
            own = ref[wide + row]
            if tile == 0:
                return own
            packed = ref[EDGE + narrow + (row + skip) // 2]
            if (row + skip) % 2:
                packed = rolled(packed, 4, 0)
            return jnp.where(sub < 2, own, packed)

        lpairs = MARGIN // 2
        for tile in range(2):
            for row in range(MARGIN):
                xs_ref[xat + row, tile] = outer(row, tile, 0, 0, 0)
            for row in range(LROWS):
                ls_ref[lat_at + row, tile] = outer(row, tile, MARGIN, lpairs, lskip)
        dpairs = lpairs + (LROWS + 1) // 2
        outer_observations(
            state,
            dat,
            lambda row, tile, outer=outer: outer(row, tile, MARGIN + LROWS, dpairs, 0),
        )
    keep = jnp.logical_not(last) | (sub < 4)
    sweep(state, 0, rows, 2 * MARGIN, keep, first & (sub < 4))
    xs_ref[MARGIN + DROWS : top - DROWS] = x3_ref[...]
    ls_ref[MARGIN + DROWS : top - DROWS] = l3_ref[...]
    sweep(state, DROWS, 0, rows + 2 * DROWS, keep)

    parts = columns // LANES
    for ref, dest in ((xs_ref, xout_ref), (ls_ref, lout_ref)):

        def gather(step, carry, ref=ref):
            value = jnp.where(
                sub < 4,
                rolled(ref[MARGIN + step, 0], 4, 0),
                rolled(ref[MARGIN + step, 1], 4, 0),
            )
            for part in range(parts):
                lines_ref[part, pl.ds(pl.multiple_of(step * SUB, SUB), SUB), :] = value[
                    :, part * LANES : (part + 1) * LANES
                ]
            return carry

        lax.fori_loop(0, rows, gather, 0, unroll=4)
        value = jnp.concatenate(
            [
                jnp.concatenate(
                    [lines_ref[part, pl.ds(slot, rows, stride=SUB), :] for part in range(parts)],
                    axis=1,
                )
                for slot in range(SUB)
            ],
            axis=0,
        )
        dest[...] = reordered(value, back=True).reshape(dest.shape)


def body(
    states,
    multipliers,
    diffusivity,
    zonal_speed,
    meridional_speed,
    observed_cells,
    observed_values,
    observed_weights,
    fresh_cells,
    fresh_values,
    fresh_weights,
):
    slots, rows, columns = states.shape
    tm_count, lat_count = lax.axis_size("tm"), lax.axis_size("lat")

    def send(value, tm_step, lat_step):
        pairs = []
        for t in range(tm_count):
            for b in range(lat_count):
                to_t, to_b = t + tm_step, b + lat_step
                if 0 <= to_t < tm_count and 0 <= to_b < lat_count:
                    pairs.append((t * lat_count + b, to_t * lat_count + to_b))
        return lax.ppermute(value, ("tm", "lat"), pairs)

    vmem = pl.BlockSpec(memory_space=pltpu.VMEM)

    def call(kernel, outs, args, scratch=(), hbm=()):
        specs = [vmem] * len(args)
        for index in hbm:
            specs[index] = pl.BlockSpec(memory_space=pl.ANY)
        return pl.pallas_call(
            kernel,
            out_shape=[jax.ShapeDtypeStruct(shape, jnp.float32) for shape in outs],
            in_specs=specs,
            out_specs=[vmem] * len(outs),
            scratch_shapes=list(scratch),
        )(*args)

    tile = (SUB, columns)
    lines = pltpu.VMEM((columns // LANES, rows * SUB, LANES), jnp.float32)
    field = (rows, *tile)
    lists = 3 * (observed_cells.shape[-1] // columns)
    coef_rows = -(-3 * MARGIN // SUB)

    def state(length):
        return (
            [pltpu.VMEM((length + 2, 2, *tile), jnp.float32)] * 6
            + [pltpu.VMEM((9, length + 2, *tile), jnp.float32)]
            + [pltpu.VMEM((12, length, columns), jnp.float32)]
        )

    obs = (observed_cells, observed_values, observed_weights)
    xl, coef = call(
        prep_kernel,
        ((2 * rows + lists, *tile), (3, rows, columns)),
        (states, multipliers, diffusivity, zonal_speed, meridional_speed, *obs),
        (lines,),
    )
    tn = send(xl, -1, 0)
    edge_rows = -(-2 * DROWS // 16) * 16
    edge_lines = pltpu.VMEM((columns // LANES, edge_rows * SUB, LANES), jnp.float32)
    up, dn, du, dd = call(
        edge_kernel,
        ([(EDGE + coef_rows, *tile)] * 2 + [(EDGE, *tile)] * 2),
        (xl, coef, *obs),
        [pltpu.VMEM((edge_rows, *tile), jnp.float32)] * 2 + [edge_lines] * 2,
    )
    lo = send(up, 0, 1)
    hi = send(dn, 0, -1)
    dlo = send(du, -1, 1)
    dhi = send(dd, -1, -1)
    obs = call(
        observation_kernel,
        (field, field, field, field),
        (tn, *obs, fresh_cells, fresh_values, fresh_weights),
        (pltpu.VMEM((lists, *tile), jnp.float32), lines, lines),
        hbm=(0,),
    )
    outer = (2 * MARGIN, 2, *tile)
    inner = (rows - 2 * DROWS, 2, *tile)
    x1, l1 = call(middle_kernel, (inner, inner), (xl, tn, *obs, coef), state(rows))
    xstrip, lstrip, up, dn, halo = call(
        strip_kernel,
        (outer, outer, *[(EDGE + PAIRS, *tile)] * 2, (3, 2 * MARGIN, columns)),
        (xl, tn, lo, hi, dlo, dhi, *obs, coef, x1, l1),
        state(2 * STRIP),
    )
    lo = send(up, 0, 1)
    hi = send(dn, 0, -1)
    x3, l3 = call(
        inner_kernel, (inner, inner), (xstrip, lstrip, x1, l1, *obs, coef), state(rows)
    )
    return tuple(
        call(
            final_kernel,
            (states.shape, states.shape),
            (xstrip, lstrip, x3, l3, lo, hi, *obs, coef, halo),
            state(rows + 2 * MARGIN) + [lines],
        )
    )


def solution(mesh):
    in_specs = (
        P("tm", "lat", None),
        P("tm", "lat", None),
        P("lat", None),
        P("lat", None),
        P("lat", None),
        P("tm", "lat", None),
        P("tm", "lat", None),
        P("tm", "lat", None),
        P(None, "lat", None),
        P(None, "lat", None),
        P(None, "lat", None),
    )
    out_specs = (P("tm", "lat", None), P("tm", "lat", None))
    return jax.shard_map(body, mesh=mesh, in_specs=in_specs, out_specs=out_specs, check_vma=False)
```

```python
import jax
import jax.numpy as jnp
from jax import lax
from jax.experimental import pallas as pl
from jax.experimental.pallas import tpu as pltpu
from jax.sharding import PartitionSpec as P

penalty_weight = 1.0
step_size = 0.15

SUB = 8
MARGIN = 12
LROWS = 9
DROWS = 6
EDGE = MARGIN + LROWS + DROWS
PAIRS = MARGIN // 2 + (LROWS + 1) // 2 + DROWS // 2
STRIP = 3 * MARGIN
LANES = 128
PIECES = 2


def rolled(value, shift, axis):
    return pltpu.roll(value, shift % value.shape[axis], axis)


def sublane(shape):
    return lax.broadcasted_iota(jnp.int32, shape, len(shape) - 2)


def two_rows(first, second):
    sub = sublane(first.shape)
    return jnp.where((sub >= 2) & (sub < 6), first, rolled(second, 4, 0))


def started(pairs, sem_ref):
    copies = [
        pltpu.make_async_copy(source, dest, sem_ref.at[index])
        for index, (source, dest) in enumerate(pairs)
    ]
    for copy in copies:
        copy.start()
    return copies


def eastward(value):
    half = value.shape[-1] // 2
    axis = value.ndim - 1
    return jnp.concatenate([value[..., half:], rolled(value[..., :half], -1, axis)], axis=axis)


def westward(value):
    half = value.shape[-1] // 2
    axis = value.ndim - 1
    return jnp.concatenate([rolled(value[..., half:], 1, axis), value[..., :half]], axis=axis)


def reordered(value, back=False):
    columns = value.shape[-1]
    natural = lax.broadcasted_iota(jnp.int32, (columns, columns), 1 if back else 0)
    parted = lax.broadcasted_iota(jnp.int32, (columns, columns), 0 if back else 1)
    target = (natural >> 1) + (natural & 1) * (columns // 2)
    moves = jnp.where(target == parted, 1.0, 0.0).astype(jnp.bfloat16)
    total = None
    for piece in reversed(split(value, 3)):
        part = jnp.dot(piece.astype(jnp.bfloat16), moves, preferred_element_type=jnp.float32)
        total = part if total is None else total + part
    return total


def interleave(lines_ref, slot, value):
    rows, columns = value.shape
    for part in range(columns // LANES):
        lines_ref[part, pl.ds(slot, rows, stride=SUB), :] = value[:, part * LANES : (part + 1) * LANES]


def copy_lines(lines_ref, dest_ref):
    rows = dest_ref.shape[0]
    for part in range(lines_ref.shape[0]):
        dest_ref[:, :, part * LANES : (part + 1) * LANES] = lines_ref[part].reshape(rows, SUB, LANES)


def prep_kernel(
    x_ref, l_ref, d_ref, z_ref, m_ref, cells_ref, values_ref, weights_ref,
    tn_ref, coef_ref, lines_ref,
):
    slots, rows, columns = x_ref.shape
    for ref, dest in ((x_ref, tn_ref.at[0:rows]), (l_ref, tn_ref.at[rows : 2 * rows])):
        value = reordered(ref[...].reshape(slots * rows, columns))
        for slot in range(slots):
            interleave(lines_ref, slot, value[slot * rows : (slot + 1) * rows])
        copy_lines(lines_ref, dest)
    for kind, ref in enumerate((d_ref, z_ref, m_ref)):
        coef_ref[kind] = reordered(ref[...])
    parts = cells_ref.shape[2] // columns
    for kind, ref in enumerate((cells_ref, values_ref, weights_ref)):
        for slot in range(slots):
            for part in range(parts):
                tn_ref[2 * rows + kind * parts + part, slot : slot + 1, :] = ref[
                    slot, :, part * columns : (part + 1) * columns
                ].astype(jnp.float32)


def split(value, count=PIECES):
    pieces = []
    for _ in range(count):
        piece = value.astype(jnp.bfloat16).astype(jnp.float32)
        pieces.append(piece)
        value = value - piece
    return pieces


def scatter(observed, slots, row_ids, columns, w_lines, v_lines):
    rows, count = row_ids.shape
    kind = jnp.bfloat16 if columns <= 256 else jnp.float32
    group = (rows // 16, 16, count)
    rows_named = row_ids.astype(jnp.float32).reshape(group).astype(kind)
    columns_named = lax.broadcasted_iota(jnp.int32, (columns, count), 0).astype(jnp.float32)
    columns_named = columns_named.reshape(columns // 16, 16, count).astype(kind)
    zero = jnp.zeros((), jnp.bfloat16)
    one = jnp.ones((1, 16, count), jnp.bfloat16)

    def spread(line, dtype):
        return jnp.broadcast_to(line.astype(jnp.float32), (16, count)).astype(dtype)[None]

    for slot in range(slots):
        cells, values, weights = observed(slot)
        row_of = cells // columns if columns & (columns - 1) else cells >> (columns.bit_length() - 1)
        column_of = cells - row_of * columns
        column_of = (column_of >> 1) + (column_of & 1) * (columns // 2)
        in_row = rows_named == spread(row_of, kind)
        left = jnp.concatenate(
            [
                jnp.where(in_row, spread(piece, jnp.bfloat16), zero).reshape(rows, count)
                for piece in split(weights) + split(weights * values)
            ],
            axis=0,
        )
        right = jnp.where(columns_named == spread(column_of, kind), one, zero)
        right = right.reshape(columns, count)
        sums = lax.dot_general(
            left, right, (((1,), (1,)), ((), ())), preferred_element_type=jnp.float32
        )
        for lines, at in ((w_lines, 0), (v_lines, PIECES)):
            total = sums[at * rows : (at + 1) * rows]
            for piece in range(1, PIECES):
                total = total + sums[(at + piece) * rows : (at + piece + 1) * rows]
            interleave(lines, slot, total)
    for slot in range(slots, SUB):
        for lines in (w_lines, v_lines):
            interleave(lines, slot, jnp.zeros((rows, columns), jnp.float32))


def edge_kernel(
    xl_ref, coef_ref, cells_ref, values_ref, weights_ref,
    up_ref, dn_ref, du_ref, dd_ref, w_ref, v_ref, w_lines, v_lines, x_ref, l_ref, sem_ref,
):
    rows, columns = coef_ref.shape[1:]
    copies = started(
        [
            (xl_ref.at[base + at : base + at + MARGIN], ref.at[out : out + MARGIN])
            for base, ref in ((0, x_ref), (rows, l_ref))
            for at, out in ((0, 0), (rows - MARGIN, MARGIN))
        ],
        sem_ref,
    )

    def observed(slot):
        return (cells_ref[slot], values_ref[slot], weights_ref[slot])

    lines = lax.broadcasted_iota(jnp.int32, (w_ref.shape[0], cells_ref.shape[2]), 0)
    row_ids = jnp.where(lines < DROWS, lines, lines + rows - 2 * DROWS)
    scatter(observed, SUB, row_ids, columns, w_lines, v_lines)
    copy_lines(w_lines, w_ref)
    copy_lines(v_lines, v_ref)
    for copy in copies:
        copy.wait()
    for ref, diag, xs, out, ls, ds, ws in (
        (up_ref, du_ref, rows - MARGIN, MARGIN, 2 * MARGIN - LROWS, 2 * MARGIN - DROWS, DROWS),
        (dn_ref, dd_ref, 0, 0, 0, 0, 0),
    ):
        for dest in (ref, diag):
            dest[0:MARGIN] = x_ref[out : out + MARGIN]
            dest[MARGIN : MARGIN + LROWS] = l_ref[ls : ls + LROWS]
            dest[MARGIN + LROWS : EDGE] = (
                v_ref[ws : ws + DROWS] - w_ref[ws : ws + DROWS] * x_ref[ds : ds + DROWS]
            )
        for kind in range(3):
            flat = coef_ref[kind, xs : xs + MARGIN, :]
            for row in range(MARGIN):
                at = kind * MARGIN + row
                ref[EDGE + at // SUB, at % SUB : at % SUB + 1, :] = flat[row : row + 1]
        for at in range(3 * MARGIN, (ref.shape[0] - EDGE) * SUB):
            ref[EDGE + at // SUB, at % SUB : at % SUB + 1, :] = jnp.zeros((1, columns), jnp.float32)


def observation_kernel(
    tn_ref, cells_ref, values_ref, weights_ref, *refs
):
    fresh, (wa_ref, va_ref, wb_ref, vb_ref, lists_ref, w_lines, v_lines) = refs[:3], refs[3:]
    last = lax.axis_index("tm") == lax.axis_size("tm") - 1
    rows, _, columns = wa_ref.shape
    pltpu.sync_copy(tn_ref.at[2 * rows : 2 * rows + lists_ref.shape[0]], lists_ref)
    parts = lists_ref.shape[0] // 3
    fresh_slots = fresh[0].shape[0]
    row_ids = lax.broadcasted_iota(jnp.int32, (rows, cells_ref.shape[2]), 0)

    def own(slot):
        return (cells_ref[slot], values_ref[slot], weights_ref[slot])

    def following(slot):
        out = []
        for kind, ref in enumerate(fresh):
            moved = jnp.concatenate(
                [lists_ref[kind * parts + part, slot : slot + 1, :] for part in range(parts)], axis=1
            )
            moved = moved.astype(ref.dtype)
            if slot < fresh_slots:
                moved = jnp.where(last, ref[slot], moved)
            elif kind == 2:
                moved = jnp.where(last, 0.0, moved)
            out.append(moved)
        return out

    scatter(own, SUB, row_ids, columns, w_lines, v_lines)
    copy_lines(w_lines, wa_ref)
    copy_lines(v_lines, va_ref)
    scatter(following, SUB - 1, row_ids, columns, w_lines, v_lines)
    copy_lines(w_lines, wb_ref)
    copy_lines(v_lines, vb_ref)


def middle_slots(first, second):
    return jnp.where(sublane(first.shape) < 4, rolled(first, 4, 0), rolled(second, 4, 0))


def slot7(value):
    return jnp.broadcast_to(value[SUB - 1 : SUB], value.shape)


def fold_coefficients(flat_ref, total, row_of):
    rows_all = lax.axis_size("lat") * row_of[1]
    diff = flat_ref[0, 0:total, :]
    zonal = 0.5 * flat_ref[1, 0:total, :]
    merid = 0.5 * flat_ref[2, 0:total, :]
    row_global = lax.axis_index("lat") * row_of[1] + row_of[0](
        lax.broadcasted_iota(jnp.int32, diff.shape, 0)
    )
    inside = (row_global >= 0) & (row_global < rows_all)
    south = diff + merid
    north = diff - merid
    east = diff - zonal
    west = diff + zonal
    planes = (
        1.0 - 4.0 * diff,
        north,
        south,
        east,
        west,
        jnp.where(inside, rolled(south, -1, 0), 0.0),
        jnp.where(inside, rolled(north, 1, 0), 0.0),
        eastward(west),
        westward(east),
    )
    for index, plane in enumerate(planes):
        flat_ref[3 + index, 0:total, :] = plane


def sweep(state, begin, stride, length, keep, frozen=None, emit=None):
    xs_ref, ls_ref, ws_ref, vs_ref, p_ref, q_ref, flat_ref = state
    sub = sublane(xs_ref.shape[2:])

    def stencil(src, adjoint, depth, finish, tiles=2):
        base = 5 if adjoint else 1
        count = length - 2 * depth
        for row in list(range(count)) + (list(range(stride, stride + count)) if stride else []):
            at = begin + depth + row
            coef = [
                jnp.broadcast_to(flat_ref[3 + k, at : at + 1, :], xs_ref.shape[2:])
                for k in (0, base, base + 1, base + 2, base + 3)
            ]
            out = []
            for tile in range(tiles):
                value = src[at, tile]
                out.append(
                    coef[0] * value
                    + coef[1] * src[at + 1, tile]
                    + coef[2] * src[at - 1, tile]
                    + coef[3] * eastward(value)
                    + coef[4] * westward(value)
                )
            finish(at, out)

    def store(dest):
        def finish(at, out):
            for tile, value in enumerate(out):
                dest[at, tile] = value

        return finish

    def forward_end(at, out):
        ahead_a = rolled(out[0], 1, 0)
        ahead_b = rolled(out[1], 1, 0)
        ahead_b = jnp.where(sub == 0, ahead_a, ahead_b)
        jump_a = jnp.where(sub == 0, 0.0, xs_ref[at, 0] - ahead_a)
        jump_b = xs_ref[at, 1] - ahead_b
        new_a = ls_ref[at, 0] + penalty_weight * jump_a
        new_b = jnp.where(keep, ls_ref[at, 1] + penalty_weight * jump_b, 0.0)
        if emit is not None:
            ls_ref[at, 1] = middle_slots(new_a, new_b)
            new_a = jnp.where(sub < 3, rolled(new_a, -5, 0), rolled(new_b, 3, 0))
            new_b = None
        ls_ref[at, 0] = new_a
        if new_b is not None:
            ls_ref[at, 1] = new_b

    def backward_end(at, out):
        back_a = rolled(out[0], -1, 0)
        back_b = rolled(out[1], -1, 0)
        back_a = jnp.where(sub == SUB - 1, back_b, back_a)
        for tile, after in ((0, back_a), (1, back_b)):
            value = xs_ref[at, tile]
            gradient = ws_ref[at, tile] * value - vs_ref[at, tile] + ls_ref[at, tile] - after
            new = value - step_size * gradient
            if frozen is not None and tile == 0:
                new = jnp.where(frozen, value, new)
            xs_ref[at, tile] = new

    def emit_end(at, out):
        value, w, v = (middle_slots(ref[at, 0], ref[at, 1]) for ref in (xs_ref, ws_ref, vs_ref))
        lagrange = ls_ref[at, 1]
        emit(at, value - step_size * (w * value - v + lagrange - out[0]), lagrange)

    tiles = 2 if emit is None else 1
    stencil(xs_ref, False, 1, store(p_ref))
    stencil(p_ref, False, 2, store(q_ref))
    stencil(q_ref, False, 3, forward_end)
    stencil(ls_ref, True, 4, store(p_ref), tiles)
    stencil(p_ref, True, 5, store(q_ref), tiles)
    stencil(q_ref, True, 6, backward_end if emit is None else emit_end, tiles)


def time_ends():
    tm = lax.axis_index("tm")
    return tm == 0, tm == lax.axis_size("tm") - 1


def own_copies(state, at, xl_ref, tn_ref, obs, first_row, count):
    xs_ref, ls_ref, ws_ref, vs_ref = state[:4]
    rows = obs[0].shape[0]
    pairs = []
    for tile, ref in ((0, xl_ref), (1, tn_ref)):
        for dest, source, start in (
            (xs_ref, ref, first_row),
            (ls_ref, ref, rows + first_row),
            (ws_ref, obs[2 * tile], first_row),
            (vs_ref, obs[2 * tile + 1], first_row),
        ):
            pairs.append((source.at[start : start + count], dest.at[at : at + count, tile]))
    return pairs


def outer_observations(state, at, rows_of):
    ws_ref, vs_ref = state[2:4]
    ws_ref[at : at + DROWS] = jnp.zeros((DROWS, *ws_ref.shape[1:]), jnp.float32)
    for row in range(DROWS):
        for tile in range(2):
            vs_ref[at + row, tile] = rows_of(row, tile)


def strip_kernel(
    xl_ref, tn_ref, lo_ref, hi_ref, dlo_ref, dhi_ref, wa_ref, va_ref, wb_ref, vb_ref, coef_ref,
    x1_ref, l1_ref, x2_ref, l2_ref, up_ref, dn_ref, halo_ref, *state,
):
    state, flat_ref, clo_ref, chi_ref, sem_ref = state[:7], *state[6:]
    xs_ref, ls_ref, ws_ref, vs_ref, p_ref = state[:5]
    rows, _, columns = wa_ref.shape
    obs = (wa_ref, va_ref, wb_ref, vb_ref)
    _, last = time_ends()
    sub = sublane((SUB, columns))
    inner = STRIP - MARGIN
    total = 2 * STRIP
    coef_copies = started(
        [(lo_ref.at[EDGE:], clo_ref), (hi_ref.at[EDGE:], chi_ref)], sem_ref.at[0:2]
    )
    pairs = own_copies(state, MARGIN, xl_ref, tn_ref, obs, 0, MARGIN)
    pairs += own_copies(state, STRIP + MARGIN, xl_ref, tn_ref, obs, rows - MARGIN, MARGIN)
    for refs, xat, lat_at, dat in (
        ((lo_ref, dlo_ref), 0, MARGIN - LROWS, MARGIN - DROWS),
        ((hi_ref, dhi_ref), STRIP + inner, STRIP + inner, STRIP + inner),
    ):
        ws_ref[dat : dat + DROWS] = jnp.zeros((DROWS, *ws_ref.shape[1:]), jnp.float32)
        for tile, ref in enumerate(refs):
            for dest, at, start, count in (
                (xs_ref, xat, 0, MARGIN),
                (ls_ref, lat_at, MARGIN, LROWS),
                (vs_ref, dat, MARGIN + LROWS, DROWS),
            ):
                pairs.append((ref.at[start : start + count], dest.at[at : at + count, tile]))
    copies = started(pairs, sem_ref.at[2:])
    for copy in coef_copies:
        copy.wait()
    for kind in range(3):
        for row in range(MARGIN):
            at = kind * MARGIN + row
            for base, ref in ((0, clo_ref), (MARGIN, chi_ref)):
                halo_ref[kind, base + row : base + row + 1, :] = ref[
                    at // SUB, at % SUB : at % SUB + 1, :
                ]
        flat_ref[kind, 0:MARGIN, :] = halo_ref[kind, 0:MARGIN, :]
        flat_ref[kind, MARGIN:STRIP, :] = coef_ref[kind, 0:inner, :]
        flat_ref[kind, STRIP : STRIP + inner, :] = coef_ref[kind, rows - inner : rows, :]
        flat_ref[kind, STRIP + inner : total, :] = halo_ref[kind, MARGIN : 2 * MARGIN, :]
    fold_coefficients(
        flat_ref,
        total,
        (lambda at: jnp.where(at < STRIP, at - MARGIN, at - STRIP + rows - inner), rows),
    )
    for copy in copies:
        copy.wait()
    keep = jnp.logical_not(last)
    sweep(state, 0, STRIP + MARGIN, 2 * MARGIN, keep)
    for dest, ref in ((xs_ref, x1_ref), (ls_ref, l1_ref)):
        count = ref.shape[0]
        dest[MARGIN + DROWS : 2 * MARGIN + DROWS] = ref[0:MARGIN]
        dest[STRIP + DROWS : STRIP + DROWS + MARGIN] = ref[count - MARGIN : count]
    sweep(state, DROWS, STRIP, 2 * MARGIN, keep)

    for ref, out, xat, lat_at, lpair, dat in (
        (dn_ref, 0, MARGIN, MARGIN, MARGIN, MARGIN),
        (
            up_ref,
            MARGIN,
            total - 2 * MARGIN,
            total - MARGIN - LROWS,
            total - MARGIN - 2 * ((LROWS + 1) // 2),
            total - MARGIN - DROWS,
        ),
    ):
        for row in range(MARGIN):
            at = xat + row
            xs_ref[at, 1] = jnp.where(last, slot7(xs_ref[at, 0]), xs_ref[at, 1])
        x2_ref[out : out + MARGIN] = xs_ref[xat : xat + MARGIN]
        l2_ref[out : out + MARGIN] = ls_ref[xat : xat + MARGIN]
        for row in range(DROWS):
            at = dat + row
            for tile in range(2):
                p_ref[at, tile] = vs_ref[at, tile] - ws_ref[at, tile] * xs_ref[at, tile]
        wide = narrow = 0
        for src, at, count, pair_at in (
            (xs_ref, xat, MARGIN, xat),
            (ls_ref, lat_at, LROWS, lpair),
            (p_ref, dat, DROWS, dat),
        ):
            for row in range(count):
                ref[wide + row] = jnp.where(sub < 2, src[at + row, 1], src[at + row, 0])
            wide += count
            for pair in range((count + 1) // 2):
                here = pair_at + 2 * pair
                ref[EDGE + narrow + pair] = two_rows(src[here, 1], src[here + 1, 1])
            narrow += (count + 1) // 2


def middle_kernel(
    xl_ref, tn_ref, wa_ref, va_ref, wb_ref, vb_ref, coef_ref, x1_ref, l1_ref, *state
):
    state, flat_ref, sem_ref = state[:7], state[6], state[7]
    xs_ref, ls_ref = state[:2]
    rows = wa_ref.shape[0]
    obs = (wa_ref, va_ref, wb_ref, vb_ref)
    copies = started(own_copies(state, 0, xl_ref, tn_ref, obs, 0, rows), sem_ref)
    _, last = time_ends()
    for kind in range(3):
        flat_ref[kind, 0:rows, :] = coef_ref[kind]
    fold_coefficients(flat_ref, rows, (lambda at: at, rows))
    for copy in copies:
        copy.wait()
    sweep(state, 0, 0, rows, jnp.logical_not(last))
    x1_ref[...] = xs_ref[DROWS : rows - DROWS]
    l1_ref[...] = ls_ref[DROWS : rows - DROWS]


def inner_kernel(
    xstrip_ref, lstrip_ref, x1_ref, l1_ref, wa_ref, va_ref, wb_ref, vb_ref, coef_ref,
    x3_ref, l3_ref, *state,
):
    state, flat_ref = state[:7], state[6]
    xs_ref, ls_ref, ws_ref, vs_ref = state[:4]
    rows, _, columns = wa_ref.shape
    first, last = time_ends()
    sub = sublane((SUB, columns))
    for kind in range(3):
        flat_ref[kind, 0:rows, :] = coef_ref[kind]
    fold_coefficients(flat_ref, rows, (lambda at: at, rows))
    for tile, w, v in ((0, wa_ref, va_ref), (1, wb_ref, vb_ref)):
        ws_ref[0:rows, tile] = w[...]
        vs_ref[0:rows, tile] = v[...]
    xs_ref[DROWS : rows - DROWS] = x1_ref[...]
    ls_ref[DROWS : rows - DROWS] = l1_ref[...]
    sweep(state, DROWS, 0, rows - 2 * DROWS, jnp.logical_not(last))

    def fix(step, carry):
        at = MARGIN + step
        xs_ref[at, 1] = jnp.where(last, slot7(xs_ref[at, 0]), xs_ref[at, 1])
        return carry

    lax.fori_loop(0, rows - 2 * MARGIN, fix, 0, unroll=4)
    for dest, strip in ((xs_ref, xstrip_ref), (ls_ref, lstrip_ref)):
        dest[0:MARGIN] = strip[0:MARGIN]
        dest[rows - MARGIN : rows] = strip[MARGIN : 2 * MARGIN]
    sweep(state, 0, 0, rows, jnp.logical_not(last) | (sub < 4), first & (sub < 4))
    x3_ref[...] = xs_ref[DROWS : rows - DROWS]
    l3_ref[...] = ls_ref[DROWS : rows - DROWS]


def final_kernel(
    xstrip_ref, lstrip_ref, x3_ref, l3_ref, lo_ref, hi_ref, wa_ref, va_ref, wb_ref, vb_ref,
    coef_ref, halo_ref, xout_ref, lout_ref, *state,
):
    state, flat_ref, lines_ref = state[:7], state[6], state[7]
    xs_ref, ls_ref, ws_ref, vs_ref = state[:4]
    rows, _, columns = wa_ref.shape
    first, last = time_ends()
    top = MARGIN + rows
    sub = sublane((SUB, columns))
    for kind in range(3):
        flat_ref[kind, 0:MARGIN, :] = halo_ref[kind, 0:MARGIN, :]
        flat_ref[kind, MARGIN:top, :] = coef_ref[kind]
        flat_ref[kind, top : top + MARGIN, :] = halo_ref[kind, MARGIN : 2 * MARGIN, :]
    fold_coefficients(flat_ref, rows + 2 * MARGIN, (lambda at: at - MARGIN, rows))
    for dest, strip in ((xs_ref, xstrip_ref), (ls_ref, lstrip_ref)):
        dest[MARGIN : 2 * MARGIN] = strip[0:MARGIN]
        dest[top - MARGIN : top] = strip[MARGIN : 2 * MARGIN]
    for tile, w, v in ((0, wa_ref, va_ref), (1, wb_ref, vb_ref)):
        ws_ref[MARGIN:top, tile] = w[...]
        vs_ref[MARGIN:top, tile] = v[...]

    for ref, xat, lat_at, lskip, dat in (
        (lo_ref, 0, MARGIN - LROWS, LROWS % 2, MARGIN - DROWS),
        (hi_ref, top, top, 0, top),
    ):

        def outer(row, tile, wide, narrow, skip, ref=ref):
            own = ref[wide + row]
            if tile == 0:
                return own
            packed = ref[EDGE + narrow + (row + skip) // 2]
            if (row + skip) % 2:
                packed = rolled(packed, 4, 0)
            return jnp.where(sub < 2, own, packed)

        lpairs = MARGIN // 2
        for tile in range(2):
            for row in range(MARGIN):
                xs_ref[xat + row, tile] = outer(row, tile, 0, 0, 0)
            for row in range(LROWS):
                ls_ref[lat_at + row, tile] = outer(row, tile, MARGIN, lpairs, lskip)
        dpairs = lpairs + (LROWS + 1) // 2
        outer_observations(
            state,
            dat,
            lambda row, tile, outer=outer: outer(row, tile, MARGIN + LROWS, dpairs, 0),
        )
    keep = jnp.logical_not(last) | (sub < 4)
    sweep(state, 0, rows, 2 * MARGIN, keep, first & (sub < 4))
    xs_ref[MARGIN + DROWS : top - DROWS] = x3_ref[...]
    ls_ref[MARGIN + DROWS : top - DROWS] = l3_ref[...]
    parts = columns // LANES

    def emit(at, new, lagrange):
        start = (at - MARGIN) * SUB
        for index, value in enumerate((new, lagrange)):
            for part in range(parts):
                lines_ref[index, part, pl.ds(start, SUB), :] = value[
                    :, part * LANES : (part + 1) * LANES
                ]

    sweep(state, DROWS, 0, rows + 2 * DROWS, keep, emit=emit)
    for index, dest in enumerate((xout_ref, lout_ref)):
        value = jnp.concatenate(
            [
                jnp.concatenate(
                    [
                        lines_ref[index, part, pl.ds(slot, rows, stride=SUB), :]
                        for part in range(parts)
                    ],
                    axis=1,
                )
                for slot in range(SUB)
            ],
            axis=0,
        )
        dest[...] = reordered(value, back=True).reshape(dest.shape)


def body(
    states,
    multipliers,
    diffusivity,
    zonal_speed,
    meridional_speed,
    observed_cells,
    observed_values,
    observed_weights,
    fresh_cells,
    fresh_values,
    fresh_weights,
):
    slots, rows, columns = states.shape
    tm_count, lat_count = lax.axis_size("tm"), lax.axis_size("lat")

    def send(value, tm_step, lat_step):
        pairs = []
        for t in range(tm_count):
            for b in range(lat_count):
                to_t, to_b = t + tm_step, b + lat_step
                if 0 <= to_t < tm_count and 0 <= to_b < lat_count:
                    pairs.append((t * lat_count + b, to_t * lat_count + to_b))
        return lax.ppermute(value, ("tm", "lat"), pairs)

    vmem = pl.BlockSpec(memory_space=pltpu.VMEM)

    def call(kernel, outs, args, scratch=(), hbm=()):
        specs = [vmem] * len(args)
        for index in hbm:
            specs[index] = pl.BlockSpec(memory_space=pltpu.HBM)
        return pl.pallas_call(
            kernel,
            out_shape=[jax.ShapeDtypeStruct(shape, jnp.float32) for shape in outs],
            in_specs=specs,
            out_specs=[vmem] * len(outs),
            scratch_shapes=list(scratch),
        )(*args)

    tile = (SUB, columns)
    lines = pltpu.VMEM((columns // LANES, rows * SUB, LANES), jnp.float32)
    field = (rows, *tile)
    lists = 3 * (observed_cells.shape[-1] // columns)
    coef_rows = -(-3 * MARGIN // SUB)

    def state(length):
        return (
            [pltpu.VMEM((length + 2, 2, *tile), jnp.float32)] * 6
            + [pltpu.VMEM((12, length, columns), jnp.float32)]
        )

    obs = (observed_cells, observed_values, observed_weights)
    xl, coef = call(
        prep_kernel,
        ((2 * rows + lists, *tile), (3, rows, columns)),
        (states, multipliers, diffusivity, zonal_speed, meridional_speed, *obs),
        (lines,),
    )
    tn = send(xl, -1, 0)
    edge_rows = -(-2 * DROWS // 16) * 16
    edge_lines = pltpu.VMEM((columns // LANES, edge_rows * SUB, LANES), jnp.float32)
    up, dn, du, dd = call(
        edge_kernel,
        ([(EDGE + coef_rows, *tile)] * 2 + [(EDGE, *tile)] * 2),
        (xl, coef, *obs),
        [pltpu.VMEM((edge_rows, *tile), jnp.float32)] * 2
        + [edge_lines] * 2
        + [pltpu.VMEM((2 * MARGIN, *tile), jnp.float32)] * 2
        + [pltpu.SemaphoreType.DMA((4,))],
        hbm=(0,),
    )
    lo = send(up, 0, 1)
    hi = send(dn, 0, -1)
    dlo = send(du, -1, 1)
    dhi = send(dd, -1, -1)
    obs = call(
        observation_kernel,
        (field, field, field, field),
        (tn, *obs, fresh_cells, fresh_values, fresh_weights),
        (pltpu.VMEM((lists, *tile), jnp.float32), lines, lines),
        hbm=(0,),
    )
    outer = (2 * MARGIN, 2, *tile)
    inner = (rows - 2 * DROWS, 2, *tile)
    x1, l1 = call(
        middle_kernel,
        (inner, inner),
        (xl, tn, *obs, coef),
        state(rows) + [pltpu.SemaphoreType.DMA((8,))],
        hbm=range(6),
    )
    xstrip, lstrip, up, dn, halo = call(
        strip_kernel,
        (outer, outer, *[(EDGE + PAIRS, *tile)] * 2, (3, 2 * MARGIN, columns)),
        (xl, tn, lo, hi, dlo, dhi, *obs, coef, x1, l1),
        state(2 * STRIP)
        + [pltpu.VMEM((coef_rows, *tile), jnp.float32)] * 2
        + [pltpu.SemaphoreType.DMA((30,))],
        hbm=range(10),
    )
    lo = send(up, 0, 1)
    hi = send(dn, 0, -1)
    x3, l3 = call(
        inner_kernel, (inner, inner), (xstrip, lstrip, x1, l1, *obs, coef), state(rows)
    )
    return tuple(
        call(
            final_kernel,
            (states.shape, states.shape),
            (xstrip, lstrip, x3, l3, lo, hi, *obs, coef, halo),
            state(rows + 2 * MARGIN)
            + [pltpu.VMEM((2, columns // LANES, rows * SUB, LANES), jnp.float32)],
        )
    )


def solution(mesh):
    in_specs = (
        P("tm", "lat", None),
        P("tm", "lat", None),
        P("lat", None),
        P("lat", None),
        P("lat", None),
        P("tm", "lat", None),
        P("tm", "lat", None),
        P("tm", "lat", None),
        P(None, "lat", None),
        P(None, "lat", None),
        P(None, "lat", None),
    )
    out_specs = (P("tm", "lat", None), P("tm", "lat", None))
    return jax.shard_map(body, mesh=mesh, in_specs=in_specs, out_specs=out_specs, check_vma=False)
```
